32 devices in a mesh: seq: 16 (over z, x, core), head: 2 (over y).
Axes of the slice: x: 2, y: 2, z: 4, core: 2. Of those that a mesh axis runs over, the one named last changes fastest.
Arguments:
- query_rows: bfloat16 [8192, 1024], P(('seq', 'head')), may hold values from -16 to 16
- key_rows: bfloat16 [8192, 1024], P(('seq', 'head')), may hold values from -16 to 16
- value_rows: bfloat16 [8192, 1024], P(('seq', 'head')), may hold values from -6 to 6
- out_grad: bfloat16 [8192, 1024], P(('seq', 'head')), may hold values from -6 to 6
- random_blocks: int32 [128, 2], P('seq'), may hold values from 0 to 127, as said below
- global_blocks: int32 [2], replicated, may hold values from 0 to 127
Outputs:
- attn_out: bfloat16 [8192, 1024], P(('seq', 'head'))
- q_grad: bfloat16 [8192, 1024], P(('seq', 'head'))
- k_grad: bfloat16 [8192, 1024], P(('seq', 'head'))
- v_grad: bfloat16 [8192, 1024], P(('seq', 'head'))
The draws below stay inside these ranges and needn't reach their ends.
Inputs may be any that keep to these rules, and one draw needn't show every extreme that they name: `random_blocks`: the 16 random blocks named by the query blocks of one device belong to 16 different devices along `seq`: at most one of them lies among any one device's 8 blocks.
All inputs are finite; a program needn't handle non-finite values.
Results may differ from the reference program's by a relative error of at most 0.011.
Values may be sent and summed in bfloat16 or wider, within the bound.
A program may use at most 128 MiB of HBM per device.

```python
import jax
import jax.numpy as jnp
from jax import lax

HEADS = 16
HEAD_DIM = 64
BLOCK = 64
RANDOM = 2
GLOBALS = 2
BLK_DEV = 8
SEQLEN = 8192
NBLK = 128
CAP = 1
N_SEQ = 16


def draw_query_rows(key, part):
    noise = jax.random.normal(jax.random.fold_in(key, 11), (SEQLEN, HEADS, HEAD_DIM), jnp.float32)
    values_drawn = jnp.clip(noise, -6.0, 6.0)
    return jnp.clip(values_drawn, -16.0, 16.0).reshape(SEQLEN, HEADS * HEAD_DIM).astype(jnp.bfloat16)


def draw_key_rows(key, part):
    noise = jax.random.normal(jax.random.fold_in(key, 13), (SEQLEN, HEADS, HEAD_DIM), jnp.float32)
    values_drawn = jnp.clip(noise, -6.0, 6.0)
    return jnp.clip(values_drawn, -16.0, 16.0).reshape(SEQLEN, HEADS * HEAD_DIM).astype(jnp.bfloat16)


def draw_random_blocks(key, part):
    slot_total = N_SEQ * CAP
    per_device = RANDOM * BLK_DEV
    device_keys = jax.random.split(jax.random.fold_in(key, 3), N_SEQ)

    def one_device(device_key):
        order = jax.random.permutation(jax.random.fold_in(device_key, 1), slot_total)[:per_device]
        source = order // CAP
        within = jax.random.randint(jax.random.fold_in(device_key, 2), (per_device,), 0, BLK_DEV)
        return (source * BLK_DEV + within).astype(jnp.int32)
    return jax.vmap(one_device)(device_keys).reshape(NBLK, RANDOM).astype(jnp.int32)


def block_levels(key, shape, pieces, smallest, high):
    loudness, own = 1.0, jax.random.fold_in(key, 6)
    for dim, parts in pieces:
        steps = jnp.exp(jax.random.uniform(jax.random.fold_in(own, dim), (parts,), jnp.float32, smallest / len(pieces), high / len(pieces)))
        loudness = loudness * jnp.repeat(steps, shape[dim] // parts).reshape([-1 if axis == dim else 1 for axis in range(len(shape))])
    return loudness


def gaussian(key, dims, width, bound, pieces=(), kind=jnp.bfloat16):
    drawn = width * jax.random.normal(key, dims, jnp.float32)
    if pieces:
        drawn = drawn * block_levels(key, dims, pieces, -0.22, 0.18)
    return jnp.clip(drawn, -bound, bound).astype(kind)


def setup_inputs(seed: int = 0) -> dict:
    streams_of = jax.random.split(jax.random.key(seed), 7)
    query_rows = draw_query_rows(jax.random.fold_in(streams_of[6], 71), 0)
    key_rows = draw_key_rows(jax.random.fold_in(streams_of[6], 71), 0)
    value_rows = gaussian(streams_of[2], (SEQLEN, HEADS * HEAD_DIM), 1.0, 6.0, ((0, 32),))
    out_grad = gaussian(streams_of[3], (SEQLEN, HEADS * HEAD_DIM), 1.0, 6.0, ((0, 32),))
    random_blocks = draw_random_blocks(jax.random.fold_in(streams_of[6], 71), 0)
    global_blocks = jax.random.randint(streams_of[5], (GLOBALS,), 0, NBLK).astype(jnp.int32)
    return dict(query_rows=query_rows, key_rows=key_rows, value_rows=value_rows, out_grad=out_grad, random_blocks=random_blocks, global_blocks=global_blocks)


masked_score = -1e30


def heads_first(matrix):
    return matrix.reshape(matrix.shape[0], HEADS, HEAD_DIM).transpose(1, 0, 2).astype(jnp.float32)


def heads_last(tensor):
    return tensor.transpose(1, 0, 2).reshape(tensor.shape[1], HEADS * HEAD_DIM)


def halfway(tensor):
    return lax.optimization_barrier(tensor.astype(jnp.bfloat16)).astype(jnp.float32)


def reference(query_rows, key_rows, value_rows, out_grad, random_blocks, global_blocks):
    full_width = HEADS * HEAD_DIM
    scale_factor = HEAD_DIM ** -0.5
    part_count = 3 + RANDOM + GLOBALS
    empty_block = jnp.zeros((1, BLOCK, full_width), jnp.bfloat16)
    key_padded = jnp.concatenate([empty_block, key_rows.reshape(NBLK, BLOCK, full_width), empty_block], axis=0)
    value_padded = jnp.concatenate([empty_block, value_rows.reshape(NBLK, BLOCK, full_width), empty_block], axis=0)
    query_blocks = query_rows.reshape(NBLK, BLOCK, full_width)
    grad_blocks = out_grad.reshape(NBLK, BLOCK, full_width)
    part_iota = jnp.arange(part_count, dtype=jnp.int32)
    random_part = (part_iota >= 3) & (part_iota < 3 + RANDOM)

    def one_block(carry, which):
        key_sum, value_sum = carry
        picked_ids = jnp.concatenate([which + jnp.arange(3, dtype=jnp.int32), random_blocks[which].astype(jnp.int32) + 1, global_blocks.astype(jnp.int32) + 1]).astype(jnp.int32)
        part_ok = jnp.ones((part_count,), jnp.bool_).at[0].set(which > 0).at[2].set(which < NBLK - 1)
        key_ok = jnp.repeat(part_ok, BLOCK)
        query_heads = heads_first(query_blocks[which])
        grad_heads = heads_first(grad_blocks[which])
        key_heads = heads_first(key_padded[picked_ids].reshape(part_count * BLOCK, full_width))
        value_heads = heads_first(value_padded[picked_ids].reshape(part_count * BLOCK, full_width))
        scores = jnp.einsum("hqd,hkd->hqk", query_heads, key_heads) * scale_factor
        scores = jnp.where(key_ok[None, None, :], scores, masked_score)
        row_max = jnp.max(scores, axis=-1, keepdims=True)
        weights_raw = jnp.exp(scores - row_max)
        probabilities = weights_raw / jnp.sum(weights_raw, axis=-1, keepdims=True)
        probs_half = halfway(probabilities)
        attended = jnp.einsum("hqk,hkd->hqd", probs_half, value_heads)
        prob_grad = jnp.einsum("hqd,hkd->hqk", grad_heads, value_heads)
        row_delta = jnp.sum(grad_heads * attended, axis=-1, keepdims=True)
        score_grad = halfway(probabilities * (prob_grad - row_delta))
        query_grad = jnp.einsum("hqk,hkd->hqd", score_grad, key_heads) * scale_factor
        key_grad = heads_last(jnp.einsum("hqk,hqd->hkd", score_grad, query_heads) * scale_factor).reshape(part_count, BLOCK, full_width)
        value_grad = heads_last(jnp.einsum("hqk,hqd->hkd", probs_half, grad_heads)).reshape(part_count, BLOCK, full_width)
        key_grad = jnp.where(random_part[:, None, None], halfway(key_grad), key_grad)
        value_grad = jnp.where(random_part[:, None, None], halfway(value_grad), value_grad)
        key_sum = key_sum.at[picked_ids].add(key_grad)
        value_sum = value_sum.at[picked_ids].add(value_grad)
        return (key_sum, value_sum), (heads_last(attended).astype(jnp.bfloat16), heads_last(query_grad).astype(jnp.bfloat16))

    start_sum = jnp.zeros((NBLK + 2, BLOCK, full_width), jnp.float32)
    (key_sum, value_sum), (attended_all, query_all) = lax.scan(one_block, (start_sum, start_sum), jnp.arange(NBLK, dtype=jnp.int32))
    attn_out = attended_all.reshape(SEQLEN, full_width)
    q_grad = query_all.reshape(SEQLEN, full_width)
    k_grad = key_sum[1:NBLK + 1].reshape(SEQLEN, full_width).astype(jnp.bfloat16)
    v_grad = value_sum[1:NBLK + 1].reshape(SEQLEN, full_width).astype(jnp.bfloat16)
    return (attn_out, q_grad, k_grad, v_grad)
```

```python
from functools import partial

import jax
import jax.numpy as jnp
from jax import lax
from jax.experimental import pallas as pl
from jax.experimental.pallas import tpu as pltpu
from jax.sharding import PartitionSpec as P

HEAD_DIM = 64
BLOCK = 64
RANDOM = 2
GLOBALS = 2
PARTS = 3 + RANDOM + GLOBALS
MASKED = -1e30
MESH = pl.DeviceIdType.MESH
VMEM = pl.BlockSpec(memory_space=pltpu.VMEM)
SMEM = pl.BlockSpec(memory_space=pltpu.SMEM)


def params(cid):
    return pltpu.CompilerParams(
        collective_id=cid, has_side_effects=True, vmem_limit_bytes=48 * 1024 * 1024
    )


def greet(n, heads):
    s, h = lax.axis_index("seq"), lax.axis_index("head")
    barrier = pltpu.get_barrier_semaphore()
    if n > 0:

        def hello(d, c):
            pl.semaphore_signal(
                barrier, inc=1, device_id={"seq": lax.rem(s + d, n)}, device_id_type=MESH
            )
            return c

        lax.fori_loop(1, n, hello, 0)
    for d in range(1, heads):
        pl.semaphore_signal(
            barrier, inc=1, device_id={"head": lax.rem(h + d, heads)}, device_id_type=MESH
        )
    pl.semaphore_wait(barrier, max(n - 1, 0) + heads - 1)


def cols(index, width, base=0):
    return pl.ds(pl.multiple_of(base + index * width, 128), width)


def rows(index, count):
    return pl.ds(pl.multiple_of(index * count, 16), count)


def each(n, f):
    def step(d, c):
        f(d)
        return c

    lax.fori_loop(1, n, step, 0)


def exchange(views, heads, send, recv, local):
    h = lax.axis_index("head")
    copies, own = [], []
    for k, view in enumerate(views):
        for d in range(1, heads):
            peer = lax.rem(h + d, heads)
            source, target = view(h, peer)
            at = k * heads + d
            copies.append(
                pltpu.make_async_remote_copy(
                    src_ref=source,
                    dst_ref=target,
                    send_sem=send.at[at],
                    recv_sem=recv.at[at],
                    device_id={"head": peer},
                    device_id_type=MESH,
                )
            )
        source, target = view(h, h)
        own.append(pltpu.make_async_copy(source, target, local.at[k]))
    return copies, own


def to_heads(src, dst, tokens, width, base=0):
    return lambda a, b: (src.at[:, cols(b, width)], dst.at[rows(a, tokens), cols(0, width, base)])


def to_tokens(src, dst, tokens, width):
    return lambda a, b: (src.at[rows(b, tokens), :], dst.at[:, cols(a, width)])


def kernel_in(n, heads, key, value, ids, pair, ids_all, send, recv, local, isend, irecv):
    s = lax.axis_index("seq")
    tokens, width = key.shape[0], key.shape[1] // heads
    greet(n, heads)
    copies, own = exchange(
        [to_heads(key, pair, tokens, width), to_heads(value, pair, tokens, width, width)],
        heads, send, recv, local,
    )

    def idc(d):
        return pltpu.make_async_remote_copy(
            src_ref=ids, dst_ref=ids_all.at[s], send_sem=isend.at[d], recv_sem=irecv.at[d],
            device_id={"seq": lax.rem(s + d, n)}, device_id_type=MESH,
        )

    mine = pltpu.make_async_copy(ids, ids_all.at[s], local.at[2])
    for c in copies:
        c.start()
    each(n, lambda d: idc(d).start())
    mine.start()
    for c in own:
        c.start()
    each(n, lambda d: idc(d).wait())
    mine.wait()
    for c in own:
        c.wait()
    for c in copies:
        c.wait()


def spread(n, src_of, dst, send, recv):
    s = lax.axis_index("seq")

    def make(d):
        peer = lax.rem(s + d, n)
        return pltpu.make_async_remote_copy(
            src_ref=src_of(peer), dst_ref=dst.at[s], send_sem=send.at[d], recv_sem=recv.at[d],
            device_id={"seq": peer}, device_id_type=MESH,
        )

    return make


def halo(n, low, high, got, send, recv):
    s = lax.axis_index("seq")
    out = []
    for k, (src, step) in enumerate(((high, 1), (low, n - 1))):
        out.append(
            pltpu.make_async_remote_copy(
                src_ref=src, dst_ref=got.at[k], send_sem=send.at[k], recv_sem=recv.at[k],
                device_id={"seq": lax.rem(s + step, n)}, device_id_type=MESH,
            )
        )
    return out


def traffic(n, heads, views, block_src, block_dst, low, high, halos, gsrc, ghere, gmine, gall,
            combine, sems):
    s = lax.axis_index("seq")
    send, recv, local, bs, br, hs, hr, gs, gr, fs, fr = sems
    greet(n, heads)
    first = spread(n, lambda p: gsrc.at[p], ghere, gs, gr)
    blocks = spread(n, lambda p: block_src.at[p], block_dst, bs, br)
    final = spread(n, lambda p: gmine, gall, fs, fr)
    edges = halo(n, low, high, halos, hs, hr)
    copies, own = exchange(views, heads, send, recv, local)
    own.append(pltpu.make_async_copy(block_src.at[s], block_dst.at[s], local.at[len(views)]))
    keep = pltpu.make_async_copy(gsrc.at[s], ghere.at[s], local.at[len(views) + 1])
    each(n, lambda d: first(d).start())
    keep.start()
    each(n, lambda d: blocks(d).start())
    for c in copies + edges + own:
        c.start()
    keep.wait()
    each(n, lambda d: first(d).wait())
    total = combine(ghere)
    gmine[...] = total
    gall[s] = total
    each(n, lambda d: final(d).start())
    for c in copies + edges + own:
        c.wait()
    each(n, lambda d: final(d).wait())
    each(n, lambda d: blocks(d).wait())


def kernel_fetch(n, heads, owners, query, grad, outgoing, pair, gcon,
                 qh, gh, incoming, halos, gall, ghere, gmine, *sems):
    tokens, width = query.shape[0], query.shape[1] // heads
    last = pair.shape[0] - BLOCK
    slot = lax.axis_index("seq") * GLOBALS // n
    traffic(
        n, heads, [to_heads(query, qh, tokens, width), to_heads(grad, gh, tokens, width)],
        outgoing, incoming, pair.at[pl.ds(0, BLOCK)], pair.at[pl.ds(last, BLOCK)], halos,
        gcon, ghere, gmine, gall, lambda ref: ref[owners[slot]], sems,
    )


def kernel_return(n, heads, att, qg, sending, edge, gsend,
                  out, qout, returned, halos, gall, ghere, gmine, *sems):
    width = att.shape[1]
    tokens = att.shape[0] // heads

    def combine(ref):
        def add(i, acc):
            return acc + ref[i].astype(jnp.float32)

        zero = jnp.zeros(ref.shape[1:], jnp.float32)
        return lax.fori_loop(0, n, add, zero).astype(jnp.bfloat16)

    traffic(
        n, heads, [to_tokens(att, out, tokens, width), to_tokens(qg, qout, tokens, width)],
        sending, returned, edge.at[0], edge.at[1], halos, gsend, ghere, gmine, gall, combine, sems,
    )


def kernel_out(heads, kg, vg, kout, vout, send, recv, local):
    width = kg.shape[1]
    tokens = kg.shape[0] // heads
    greet(0, heads)
    copies, own = exchange(
        [to_tokens(kg, kout, tokens, width), to_tokens(vg, vout, tokens, width)],
        heads, send, recv, local,
    )
    for c in copies + own:
        c.start()
    for c in own + copies:
        c.wait()


def dot(a, b, ca, cb):
    return lax.dot_general(a, b, (((ca,), (cb,)), ((), ())), preferred_element_type=jnp.float32)


def kernel_attend(n, lanes, slots, qh, gh, pair, halos, incoming, gall,
                  att, qg, wsum, edge, sending, gsum, pairs, keys, gacc):
    nb = qh.shape[0] // BLOCK
    width = qh.shape[1]
    s = lax.axis_index("seq")
    per = lanes // HEAD_DIM
    scale = HEAD_DIM ** (-0.5)
    pairs[pl.ds(0, BLOCK)] = halos[0]
    pairs[pl.ds(BLOCK, nb * BLOCK)] = pair[...]
    pairs[pl.ds((nb + 1) * BLOCK, BLOCK)] = halos[1]
    keys[pl.ds((3 + RANDOM) * BLOCK, GLOBALS * BLOCK)] = gall[...]
    gacc[...] = jnp.zeros_like(gacc)
    wsum[...] = jnp.zeros_like(wsum)
    if n > RANDOM * nb:
        sending[...] = jnp.zeros_like(sending)
    lane_head = lax.broadcasted_iota(jnp.int32, (BLOCK, lanes), 1) // HEAD_DIM
    part = lax.broadcasted_iota(jnp.int32, (1, PARTS * BLOCK), 1) // BLOCK

    def stack(x):
        zero = jnp.zeros_like(x)
        return jnp.concatenate([jnp.where(lane_head == j, x, zero) for j in range(per)], axis=0)

    def unstack(x):
        got = x[0:BLOCK]
        for j in range(1, per):
            got = jnp.where(lane_head == j, x[j * BLOCK : (j + 1) * BLOCK], got)
        return got

    def block(b, carry):
        here = pl.ds(pl.multiple_of(b * BLOCK, BLOCK), BLOCK)
        window = pl.ds(pl.multiple_of(b * BLOCK, BLOCK), 3 * BLOCK)
        keys[pl.ds(0, 3 * BLOCK)] = pairs[window]
        for r in range(RANDOM):
            keys[pl.ds((3 + r) * BLOCK, BLOCK)] = incoming[slots[b * RANDOM + r]]
        number = s * nb + b
        bad = ((part == 0) & (number == 0)) | ((part == 2) & (number == n * nb - 1))
        for g in range(width // lanes):
            at = pl.ds(g * lanes, lanes)
            vat = pl.ds(width + g * lanes, lanes)
            q = stack(qh[here, at])
            do = stack(gh[here, at])
            k = keys[:, at]
            v = keys[:, vat]
            scores = jnp.where(bad, MASKED, dot(q, k, 1, 1) * scale)
            raw = jnp.exp(scores - jnp.max(scores, axis=-1, keepdims=True))
            probs = raw * (1.0 / jnp.sum(raw, axis=-1, keepdims=True))
            half = probs.astype(jnp.bfloat16)
            attended = dot(half, v, 1, 0)
            delta = jnp.sum(do.astype(jnp.float32) * attended, axis=-1, keepdims=True)
            ds = (probs * (dot(do, v, 1, 1) - delta)).astype(jnp.bfloat16)
            att[here, at] = unstack(attended).astype(jnp.bfloat16)
            qg[here, at] = (unstack(dot(ds, k, 1, 0)) * scale).astype(jnp.bfloat16)
            for x, y, to, mult in ((ds, q, at, scale), (half, do, vat, 1.0)):
                grad = dot(x, y, 0, 0) * mult
                wsum[window, to] += grad[: 3 * BLOCK]
                for r in range(RANDOM):
                    low = (3 + r) * BLOCK
                    sending[slots[b * RANDOM + r], :, to] = grad[low : low + BLOCK].astype(
                        jnp.bfloat16
                    )
                gacc[:, to] += grad[(3 + RANDOM) * BLOCK :]
        return carry

    lax.fori_loop(0, nb, block, 0)
    edge[0] = wsum[pl.ds(0, BLOCK)].astype(jnp.bfloat16)
    edge[1] = wsum[pl.ds((nb + 1) * BLOCK, BLOCK)].astype(jnp.bfloat16)
    gsum[...] = gacc[...].astype(jnp.bfloat16)


def kernel_sum(n, served, owners, owned_at, wsum, halos, returned, gall, kg, vg, acc):
    nb = kg.shape[0] // BLOCK
    width = kg.shape[1]
    s = lax.axis_index("seq")
    acc[...] = wsum[pl.ds(BLOCK, nb * BLOCK)]
    acc[pl.ds(0, BLOCK)] += halos[0].astype(jnp.float32)
    acc[pl.ds((nb - 1) * BLOCK, BLOCK)] += halos[1].astype(jnp.float32)

    def add(i, c):
        at = pl.ds(pl.multiple_of(served[i] * BLOCK, BLOCK), BLOCK)
        acc[at] += returned[i].astype(jnp.float32)
        return c

    lax.fori_loop(0, n, add, 0)
    for g in range(GLOBALS):

        @pl.when(owners[g] == s)
        def _():
            at = pl.ds(pl.multiple_of(owned_at[g] * BLOCK, BLOCK), BLOCK)
            acc[at] += gall[pl.ds(g * BLOCK, BLOCK)].astype(jnp.float32)

    kg[...] = acc[:, pl.ds(0, width)].astype(jnp.bfloat16)
    vg[...] = acc[:, pl.ds(width, width)].astype(jnp.bfloat16)


def body(n, heads, query_rows, key_rows, value_rows, out_grad, random_blocks, global_blocks):
    bf = jnp.bfloat16
    tokens, full = query_rows.shape
    width = full // heads
    total = tokens * heads
    nb = total // BLOCK
    me = lax.axis_index("seq")
    dma = pltpu.SemaphoreType.DMA
    sds = jax.ShapeDtypeStruct
    requests = RANDOM * nb
    flat = random_blocks.reshape(requests)
    ids = jnp.broadcast_to(jnp.pad(flat, (0, 128 - requests))[None], (8, 128))
    pair, ids_all = pl.pallas_call(
        partial(kernel_in, n, heads),
        out_shape=(sds((total, 2 * width), bf), sds((n, 8, 128), jnp.int32)),
        in_specs=[VMEM] * 3,
        out_specs=(VMEM,) * 2,
        scratch_shapes=[dma((2 * heads,)), dma((2 * heads,)), dma((3,)), dma((n,)), dma((n,))],
        compiler_params=params(0),
        name="head_in",
    )(key_rows, value_rows, ids)
    asked = ids_all[:, 0, :requests]
    served = jnp.sum(jnp.where(asked // nb == me, asked % nb, 0), axis=1).astype(jnp.int32)
    owners = global_blocks // nb
    owned_at = global_blocks % nb
    pair_blocks = pair.reshape(nb, BLOCK, 2 * width)
    outgoing = jnp.take(pair_blocks, served, axis=0, mode="clip")
    chunk = GLOBALS * BLOCK // n
    gcon = jnp.take(pair_blocks, owned_at, axis=0, mode="clip").reshape(n, chunk, 2 * width)
    slab = sds((n, BLOCK, 2 * width), bf)
    small = sds((n, chunk, 2 * width), bf)
    sems = [dma((2 * heads,)), dma((2 * heads,)), dma((4,)), dma((n,)), dma((n,)),
            dma((2,)), dma((2,)), dma((n,)), dma((n,)), dma((n,)), dma((n,))]
    scratch = [pltpu.VMEM(small.shape, bf), pltpu.VMEM(small.shape[1:], bf)] + sems
    edges = sds((2, BLOCK, 2 * width), bf)
    qh, gh, incoming, halos, gall = pl.pallas_call(
        partial(kernel_fetch, n, heads),
        out_shape=(sds((total, width), bf), sds((total, width), bf), slab, edges, small),
        in_specs=[SMEM] + [VMEM] * 5,
        out_specs=(VMEM,) * 5,
        scratch_shapes=scratch,
        compiler_params=params(1),
        name="fetch",
    )(owners, query_rows, out_grad, outgoing, pair, gcon)
    gwide = (GLOBALS * BLOCK, 2 * width)
    att, qg, wsum, edge, sending, gsum = pl.pallas_call(
        partial(kernel_attend, n, min(256, width)),
        out_shape=(
            sds((total, width), bf), sds((total, width), bf),
            sds(((nb + 2) * BLOCK, 2 * width), jnp.float32), edges, slab, sds(gwide, bf),
        ),
        in_specs=[SMEM] + [VMEM] * 6,
        out_specs=(VMEM,) * 6,
        scratch_shapes=[
            pltpu.VMEM(((nb + 2) * BLOCK, 2 * width), bf),
            pltpu.VMEM((PARTS * BLOCK, 2 * width), bf),
            pltpu.VMEM(gwide, jnp.float32),
        ],
        compiler_params=pltpu.CompilerParams(vmem_limit_bytes=48 * 1024 * 1024),
        name="attend",
    )(flat // nb, qh, gh, pair, halos, incoming, gall.reshape(gwide))
    out, qout, returned, back, gtot = pl.pallas_call(
        partial(kernel_return, n, heads),
        out_shape=(sds((tokens, full), bf), sds((tokens, full), bf), slab, edges, small),
        in_specs=[VMEM] * 5,
        out_specs=(VMEM,) * 5,
        scratch_shapes=scratch,
        compiler_params=params(2),
        name="give_back",
    )(att, qg, sending, edge, gsum.reshape(n, chunk, 2 * width))
    kg, vg = pl.pallas_call(
        partial(kernel_sum, n),
        out_shape=(sds((total, width), bf),) * 2,
        in_specs=[SMEM] * 3 + [VMEM] * 4,
        out_specs=(VMEM,) * 2,
        scratch_shapes=[pltpu.VMEM((total, 2 * width), jnp.float32)],
        compiler_params=pltpu.CompilerParams(vmem_limit_bytes=48 * 1024 * 1024),
        name="sum_owned",
    )(served, owners, owned_at, wsum, back, returned, gtot.reshape(gwide))
    kout, vout = pl.pallas_call(
        partial(kernel_out, heads),
        out_shape=(sds((tokens, full), bf),) * 2,
        in_specs=[VMEM] * 2,
        out_specs=(VMEM,) * 2,
        scratch_shapes=[dma((2 * heads,)), dma((2 * heads,)), dma((2,))],
        compiler_params=params(3),
        name="head_out",
    )(kg, vg)
    return out, qout, kout, vout


def solution(mesh):
    rows_spec = P(("seq", "head"), None)
    return jax.shard_map(
        partial(body, mesh.shape["seq"], mesh.shape["head"]),
        mesh=mesh,
        in_specs=(rows_spec,) * 4 + (P("seq", None), P()),
        out_specs=(rows_spec,) * 4,
        check_vma=False,
    )
```

```python
from functools import partial

import jax
import jax.numpy as jnp
from jax import lax
from jax.experimental import pallas as pl
from jax.experimental.pallas import tpu as pltpu
from jax.sharding import PartitionSpec as P

HEAD_DIM = 64
BLOCK = 64
RANDOM = 2
GLOBALS = 2
PARTS = 3 + RANDOM + GLOBALS
MASKED = -1e30
MESH = pl.DeviceIdType.MESH
VMEM = pl.BlockSpec(memory_space=pltpu.VMEM)
ANY = pl.BlockSpec(memory_space=pl.ANY)
SMEM = pl.BlockSpec(memory_space=pltpu.SMEM)


def params(cid):
    return pltpu.CompilerParams(
        collective_id=cid, has_side_effects=True, vmem_limit_bytes=48 * 1024 * 1024
    )


def greet(n, heads):
    s, h = lax.axis_index("seq"), lax.axis_index("head")
    barrier = pltpu.get_barrier_semaphore()
    if n > 0:

        def hello(d, c):
            pl.semaphore_signal(
                barrier, inc=1, device_id={"seq": lax.rem(s + d, n)}, device_id_type=MESH
            )
            return c

        lax.fori_loop(1, n, hello, 0)
    for d in range(1, heads):
        pl.semaphore_signal(
            barrier, inc=1, device_id={"head": lax.rem(h + d, heads)}, device_id_type=MESH
        )
    pl.semaphore_wait(barrier, max(n - 1, 0) + heads - 1)


def cols(index, width, base=0):
    return pl.ds(pl.multiple_of(base + index * width, 128), width)


def rows(index, count):
    return pl.ds(pl.multiple_of(index * count, 16), count)


def each(n, f):
    def step(d, c):
        f(d)
        return c

    lax.fori_loop(1, n, step, 0)


def exchange(views, heads, send, recv, local):
    h = lax.axis_index("head")
    copies, own = [], []
    for k, view in enumerate(views):
        for d in range(1, heads):
            peer = lax.rem(h + d, heads)
            source, target = view(h, peer)
            at = k * heads + d
            copies.append(
                pltpu.make_async_remote_copy(
                    src_ref=source,
                    dst_ref=target,
                    send_sem=send.at[at],
                    recv_sem=recv.at[at],
                    device_id={"head": peer},
                    device_id_type=MESH,
                )
            )
        source, target = view(h, h)
        own.append(pltpu.make_async_copy(source, target, local.at[k]))
    return copies, own


def to_heads(src, dst, tokens, width, base=0):
    return lambda a, b: (src.at[:, cols(b, width)], dst.at[rows(a, tokens), cols(0, width, base)])


def to_tokens(src, dst, tokens, width):
    return lambda a, b: (src.at[rows(b, tokens), :], dst.at[:, cols(a, width)])


def kernel_in(n, heads, key, value, ids, pair, ids_all, send, recv, local, isend, irecv):
    s = lax.axis_index("seq")
    tokens, width = key.shape[0], key.shape[1] // heads
    greet(n, heads)
    copies, own = exchange(
        [to_heads(key, pair, tokens, width), to_heads(value, pair, tokens, width, width)],
        heads, send, recv, local,
    )

    def idc(d):
        return pltpu.make_async_remote_copy(
            src_ref=ids, dst_ref=ids_all.at[s], send_sem=isend.at[d], recv_sem=irecv.at[d],
            device_id={"seq": lax.rem(s + d, n)}, device_id_type=MESH,
        )

    mine = pltpu.make_async_copy(ids, ids_all.at[s], local.at[2])
    for c in copies:
        c.start()
    each(n, lambda d: idc(d).start())
    mine.start()
    for c in own:
        c.start()
    each(n, lambda d: idc(d).wait())
    mine.wait()
    for c in own:
        c.wait()
    for c in copies:
        c.wait()


def spread(n, src_of, dst, send, recv):
    s = lax.axis_index("seq")

    def make(d):
        peer = lax.rem(s + d, n)
        return pltpu.make_async_remote_copy(
            src_ref=src_of(peer), dst_ref=dst.at[s], send_sem=send.at[d], recv_sem=recv.at[d],
            device_id={"seq": peer}, device_id_type=MESH,
        )

    return make


def halo(n, low, high, got, send, recv):
    s = lax.axis_index("seq")
    out = []
    for k, (src, step) in enumerate(((high, 1), (low, n - 1))):
        out.append(
            pltpu.make_async_remote_copy(
                src_ref=src, dst_ref=got.at[k], send_sem=send.at[k], recv_sem=recv.at[k],
                device_id={"seq": lax.rem(s + step, n)}, device_id_type=MESH,
            )
        )
    return out


def traffic(n, heads, views, block_src, block_dst, low, high, halos, gsrc, ghere, gmine, glayer,
            gdone, gall, first, second, sems):
    s = lax.axis_index("seq")
    send, recv, local, bs, br, hs, hr, gs, gr, ls, lr, fs, fr = sems
    group = gsrc.shape[0]
    layers = n // group
    mine, layer = lax.rem(s, group), s // group
    greet(n, heads)
    blocks = spread(n, lambda p: block_src.at[p], block_dst, bs, br)
    edges = halo(n, low, high, halos, hs, hr)
    copies, own = exchange(views, heads, send, recv, local)
    own.append(pltpu.make_async_copy(block_src.at[s], block_dst.at[s], local.at[len(views)]))
    keep = pltpu.make_async_copy(gsrc.at[mine], ghere.at[mine], local.at[len(views) + 1])

    def inside(src_of, dst, ss, rs):
        out = []
        for j in range(1, group):
            to = lax.rem(mine + j, group)
            out.append(
                pltpu.make_async_remote_copy(
                    src_ref=src_of(to), dst_ref=dst.at[mine], send_sem=ss.at[j],
                    recv_sem=rs.at[j], device_id={"seq": layer * group + to},
                    device_id_type=MESH,
                )
            )
        return out

    def across(j):
        return pltpu.make_async_remote_copy(
            src_ref=gmine, dst_ref=glayer.at[layer], send_sem=ls.at[j], recv_sem=lr.at[j],
            device_id={"seq": lax.rem(layer + j, layers) * group + mine}, device_id_type=MESH,
        )

    def distance(i):
        return n // 2 + ((i + 1) // 2) * (2 * lax.rem(i, 2) - 1)

    def go(i, c):
        blocks(distance(i)).start()
        return c

    step1 = inside(lambda to: gsrc.at[to], ghere, gs, gr)
    step3 = inside(lambda to: gdone, gall, fs, fr)
    for c in step1 + [keep]:
        c.start()
    lax.fori_loop(0, n // 2, go, 0)
    for c in copies + edges + own:
        c.start()
    for c in step1 + [keep]:
        c.wait()
    part = first(ghere)
    gmine[...] = part
    glayer[layer] = part
    each(layers, lambda j: across(j).start())
    lax.fori_loop(n // 2, n - 1, go, 0)
    for c in copies + edges + own:
        c.wait()
    each(layers, lambda j: across(j).wait())
    total = second(glayer)
    gdone[...] = total
    gall[mine] = total
    for c in step3:
        c.start()
    for c in step3:
        c.wait()
    each(n, lambda d: blocks(d).wait())


def kernel_fetch(n, heads, owners, query, grad, outgoing, pair, gcon,
                 qh, gh, incoming, halos, gall, ghere, gmine, glayer, gdone, *sems):
    tokens, width = query.shape[0], query.shape[1] // heads
    last = pair.shape[0] - BLOCK
    group = gcon.shape[0]
    slot = lax.rem(lax.axis_index("seq"), group) * GLOBALS // group
    traffic(
        n, heads, [to_heads(query, qh, tokens, width), to_heads(grad, gh, tokens, width)],
        outgoing, incoming, pair.at[pl.ds(0, BLOCK)], pair.at[pl.ds(last, BLOCK)], halos,
        gcon, ghere, gmine, glayer, gdone, gall,
        lambda ref: ref[lax.rem(owners[slot], group)], lambda ref: ref[owners[slot] // group],
        sems,
    )


def kernel_return(n, heads, att, qg, sending, edge, gsend,
                  out, qout, returned, halos, gall, ghere, gmine, glayer, gdone, *sems):
    width = att.shape[1]
    tokens = att.shape[0] // heads

    def combine(ref):
        def add(i, acc):
            return acc + ref[i].astype(jnp.float32)

        zero = jnp.zeros(ref.shape[1:], jnp.float32)
        return lax.fori_loop(0, ref.shape[0], add, zero).astype(jnp.bfloat16)

    traffic(
        n, heads, [to_tokens(att, out, tokens, width), to_tokens(qg, qout, tokens, width)],
        sending, returned, edge.at[0], edge.at[1], halos, gsend, ghere, gmine, glayer, gdone,
        gall, combine, combine, sems,
    )


def kernel_out(heads, kg, vg, kout, vout, send, recv, local):
    width = kg.shape[1]
    tokens = kg.shape[0] // heads
    greet(0, heads)
    copies, own = exchange(
        [to_tokens(kg, kout, tokens, width), to_tokens(vg, vout, tokens, width)],
        heads, send, recv, local,
    )
    for c in copies + own:
        c.start()
    for c in own + copies:
        c.wait()


def dot(a, b, ca, cb):
    return lax.dot_general(a, b, (((ca,), (cb,)), ((), ())), preferred_element_type=jnp.float32)


def kernel_attend(n, lanes, slots, qh, gh, pair, halos, incoming, gall,
                  att, qg, wsum, edge, sending, gsum, pairs, keys, gacc):
    nb = qh.shape[0] // BLOCK
    width = qh.shape[1]
    s = lax.axis_index("seq")
    per = lanes // HEAD_DIM
    scale = jnp.asarray(HEAD_DIM ** (-0.5), jnp.bfloat16)
    pairs[pl.ds(0, BLOCK)] = halos[0]
    pairs[pl.ds(BLOCK, nb * BLOCK)] = pair[...]
    pairs[pl.ds((nb + 1) * BLOCK, BLOCK)] = halos[1]
    keys[pl.ds((3 + RANDOM) * BLOCK, GLOBALS * BLOCK)] = gall[...]
    gacc[...] = jnp.zeros_like(gacc)
    wsum[...] = jnp.zeros_like(wsum)
    if n > RANDOM * nb:
        sending[...] = jnp.zeros_like(sending)
    lane_head = lax.broadcasted_iota(jnp.int32, (BLOCK, lanes), 1) // HEAD_DIM
    part = lax.broadcasted_iota(jnp.int32, (PARTS * BLOCK, 1), 0) // BLOCK

    def stack(x):
        zero = jnp.zeros_like(x)
        return jnp.concatenate([jnp.where(lane_head == j, x, zero) for j in range(per)], axis=0)

    def unstack(x):
        got = x[0:BLOCK]
        for j in range(1, per):
            got = jnp.where(lane_head == j, x[j * BLOCK : (j + 1) * BLOCK], got)
        return got

    def block(b, carry):
        here = pl.ds(pl.multiple_of(b * BLOCK, BLOCK), BLOCK)
        window = pl.ds(pl.multiple_of(b * BLOCK, BLOCK), 3 * BLOCK)
        keys[pl.ds(0, 3 * BLOCK)] = pairs[window]
        for r in range(RANDOM):
            keys[pl.ds((3 + r) * BLOCK, BLOCK)] = incoming[slots[b * RANDOM + r]]
        number = s * nb + b
        bad = ((part == 0) & (number == 0)) | ((part == 2) & (number == n * nb - 1))
        for g in range(width // lanes):
            at = pl.ds(g * lanes, lanes)
            vat = pl.ds(width + g * lanes, lanes)
            q = stack(qh[here, at]) * scale
            do = stack(gh[here, at])
            k = keys[:, at]
            v = keys[:, vat]
            scores = jnp.where(bad, MASKED, dot(k, q, 1, 1))
            raw = jnp.exp(scores - jnp.max(scores, axis=0, keepdims=True))
            probs = raw * (1.0 / jnp.sum(raw, axis=0, keepdims=True))
            half = probs.astype(jnp.bfloat16)
            pgrad = dot(v, do, 1, 1)
            delta = jnp.sum(half.astype(jnp.float32) * pgrad, axis=0, keepdims=True)
            ds = (probs * (pgrad - delta)).astype(jnp.bfloat16)
            att[here, at] = unstack(dot(half, v, 0, 0)).astype(jnp.bfloat16)
            qg[here, at] = (unstack(dot(ds, k, 0, 0)) * HEAD_DIM ** (-0.5)).astype(jnp.bfloat16)
            for x, y, to in ((ds, q, at), (half, do, vat)):
                grad = dot(x, y, 1, 0)
                wsum[window, to] += grad[: 3 * BLOCK]
                for r in range(RANDOM):
                    low = (3 + r) * BLOCK
                    sending[slots[b * RANDOM + r], :, to] = grad[low : low + BLOCK].astype(
                        jnp.bfloat16
                    )
                gacc[:, to] += grad[(3 + RANDOM) * BLOCK :]
        return carry

    lax.fori_loop(0, nb, block, 0)
    edge[0] = wsum[pl.ds(0, BLOCK)].astype(jnp.bfloat16)
    edge[1] = wsum[pl.ds((nb + 1) * BLOCK, BLOCK)].astype(jnp.bfloat16)
    gsum[...] = gacc[...].astype(jnp.bfloat16)


def kernel_sum(n, served, owners, owned_at, wsum, halos, returned, gall, kg, vg, acc):
    nb = kg.shape[0] // BLOCK
    width = kg.shape[1]
    s = lax.axis_index("seq")
    acc[...] = wsum[pl.ds(BLOCK, nb * BLOCK)]
    acc[pl.ds(0, BLOCK)] += halos[0].astype(jnp.float32)
    acc[pl.ds((nb - 1) * BLOCK, BLOCK)] += halos[1].astype(jnp.float32)

    def add(i, c):
        at = pl.ds(pl.multiple_of(served[i] * BLOCK, BLOCK), BLOCK)
        acc[at] += returned[i].astype(jnp.float32)
        return c

    lax.fori_loop(0, n, add, 0)
    for g in range(GLOBALS):

        @pl.when(owners[g] == s)
        def _():
            at = pl.ds(pl.multiple_of(owned_at[g] * BLOCK, BLOCK), BLOCK)
            acc[at] += gall[pl.ds(g * BLOCK, BLOCK)].astype(jnp.float32)

    kg[...] = acc[:, pl.ds(0, width)].astype(jnp.bfloat16)
    vg[...] = acc[:, pl.ds(width, width)].astype(jnp.bfloat16)


def body(n, heads, query_rows, key_rows, value_rows, out_grad, random_blocks, global_blocks):
    bf = jnp.bfloat16
    tokens, full = query_rows.shape
    width = full // heads
    total = tokens * heads
    nb = total // BLOCK
    me = lax.axis_index("seq")
    dma = pltpu.SemaphoreType.DMA
    sds = jax.ShapeDtypeStruct
    requests = RANDOM * nb
    flat = random_blocks.reshape(requests)
    ids = jnp.broadcast_to(jnp.pad(flat, (0, 128 - requests))[None], (8, 128))
    pair, ids_all = pl.pallas_call(
        partial(kernel_in, n, heads),
        out_shape=(sds((total, 2 * width), bf), sds((n, 8, 128), jnp.int32)),
        in_specs=[ANY, ANY, VMEM],
        out_specs=(VMEM,) * 2,
        scratch_shapes=[dma((2 * heads,)), dma((2 * heads,)), dma((3,)), dma((n,)), dma((n,))],
        compiler_params=params(0),
        name="head_in",
    )(key_rows, value_rows, ids)
    asked = ids_all[:, 0, :requests]
    served = jnp.sum(jnp.where(asked // nb == me, asked % nb, 0), axis=1).astype(jnp.int32)
    owners = global_blocks // nb
    owned_at = global_blocks % nb
    pair_blocks = pair.reshape(nb, BLOCK, 2 * width)
    outgoing = jnp.take(pair_blocks, served, axis=0, mode="clip")
    group = 4
    layers = n // group
    chunk = GLOBALS * BLOCK // group
    gcon = jnp.take(pair_blocks, owned_at, axis=0, mode="clip").reshape(group, chunk, 2 * width)
    slab = sds((n, BLOCK, 2 * width), bf)
    small = sds((group, chunk, 2 * width), bf)
    sems = [dma((2 * heads,)), dma((2 * heads,)), dma((4,)), dma((n,)), dma((n,)),
            dma((2,)), dma((2,)), dma((group,)), dma((group,)), dma((layers,)), dma((layers,)),
            dma((group,)), dma((group,))]
    wide = (chunk, 2 * width)
    scratch = [pltpu.VMEM(small.shape, bf), pltpu.VMEM(wide, bf),
               pltpu.VMEM((layers,) + wide, bf), pltpu.VMEM(wide, bf)] + sems
    edges = sds((2, BLOCK, 2 * width), bf)
    qh, gh, incoming, halos, gall = pl.pallas_call(
        partial(kernel_fetch, n, heads),
        out_shape=(sds((total, width), bf), sds((total, width), bf), slab, edges, small),
        in_specs=[SMEM, ANY, ANY] + [VMEM] * 3,
        out_specs=(VMEM,) * 5,
        scratch_shapes=scratch,
        compiler_params=params(1),
        name="fetch",
    )(owners, query_rows, out_grad, outgoing, pair, gcon)
    gwide = (GLOBALS * BLOCK, 2 * width)
    att, qg, wsum, edge, sending, gsum = pl.pallas_call(
        partial(kernel_attend, n, min(256, width)),
        out_shape=(
            sds((total, width), bf), sds((total, width), bf),
            sds(((nb + 2) * BLOCK, 2 * width), jnp.float32), edges, slab, sds(gwide, bf),
        ),
        in_specs=[SMEM] + [VMEM] * 6,
        out_specs=(VMEM,) * 6,
        scratch_shapes=[
            pltpu.VMEM(((nb + 2) * BLOCK, 2 * width), bf),
            pltpu.VMEM((PARTS * BLOCK, 2 * width), bf),
            pltpu.VMEM(gwide, jnp.float32),
        ],
        compiler_params=pltpu.CompilerParams(vmem_limit_bytes=48 * 1024 * 1024),
        name="attend",
    )(flat // nb, qh, gh, pair, halos, incoming, gall.reshape(gwide))
    out, qout, returned, back, gtot = pl.pallas_call(
        partial(kernel_return, n, heads),
        out_shape=(sds((tokens, full), bf), sds((tokens, full), bf), slab, edges, small),
        in_specs=[VMEM] * 5,
        out_specs=(VMEM,) * 5,
        scratch_shapes=scratch,
        compiler_params=params(2),
        name="give_back",
    )(att, qg, sending, edge, gsum.reshape(group, chunk, 2 * width))
    kg, vg = pl.pallas_call(
        partial(kernel_sum, n),
        out_shape=(sds((total, width), bf),) * 2,
        in_specs=[SMEM] * 3 + [VMEM] * 4,
        out_specs=(VMEM,) * 2,
        scratch_shapes=[pltpu.VMEM((total, 2 * width), jnp.float32)],
        compiler_params=pltpu.CompilerParams(vmem_limit_bytes=48 * 1024 * 1024),
        name="sum_owned",
    )(served, owners, owned_at, wsum, back, returned, gtot.reshape(gwide))
    kout, vout = pl.pallas_call(
        partial(kernel_out, heads),
        out_shape=(sds((tokens, full), bf),) * 2,
        in_specs=[VMEM] * 2,
        out_specs=(VMEM,) * 2,
        scratch_shapes=[dma((2 * heads,)), dma((2 * heads,)), dma((2,))],
        compiler_params=params(3),
        name="head_out",
    )(kg, vg)
    return out, qout, kout, vout


def solution(mesh):
    rows_spec = P(("seq", "head"), None)
    return jax.shard_map(
        partial(body, mesh.shape["seq"], mesh.shape["head"]),
        mesh=mesh,
        in_specs=(rows_spec,) * 4 + (P("seq", None), P()),
        out_specs=(rows_spec,) * 4,
        check_vma=False,
    )
```

```python
from functools import partial

import jax
import jax.numpy as jnp
from jax import lax
from jax.experimental import pallas as pl
from jax.experimental.pallas import tpu as pltpu
from jax.sharding import PartitionSpec as P

HEAD_DIM = 64
BLOCK = 64
RANDOM = 2
GLOBALS = 2
PARTS = 3 + RANDOM + GLOBALS
MASKED = -1e30
MESH = pl.DeviceIdType.MESH
VMEM = pl.BlockSpec(memory_space=pltpu.VMEM)
HBM = pl.BlockSpec(memory_space=pltpu.HBM)
SMEM = pl.BlockSpec(memory_space=pltpu.SMEM)


def params(cid):
    return pltpu.CompilerParams(
        collective_id=cid, has_side_effects=True, vmem_limit_bytes=48 * 1024 * 1024
    )


def greet(n, heads):
    s, h = lax.axis_index("seq"), lax.axis_index("head")
    barrier = pltpu.get_barrier_semaphore()
    if n > 0:

        def hello(d, c):
            pl.semaphore_signal(
                barrier, inc=1, device_id={"seq": lax.rem(s + d, n)}, device_id_type=MESH
            )
            return c

        lax.fori_loop(1, n, hello, 0)
    for d in range(1, heads):
        pl.semaphore_signal(
            barrier, inc=1, device_id={"head": lax.rem(h + d, heads)}, device_id_type=MESH
        )
    pl.semaphore_wait(barrier, max(n - 1, 0) + heads - 1)


def cols(index, width, base=0):
    return pl.ds(pl.multiple_of(base + index * width, 128), width)


def rows(index, count):
    return pl.ds(pl.multiple_of(index * count, 16), count)


def each(n, f):
    def step(d, c):
        f(d)
        return c

    lax.fori_loop(1, n, step, 0)


def remote(src, dst, send, recv, **where):
    return pltpu.make_async_remote_copy(
        src_ref=src, dst_ref=dst, send_sem=send, recv_sem=recv, device_id=where,
        device_id_type=MESH,
    )


def exchange(view, heads, send, recv, local, base):
    h = lax.axis_index("head")
    copies = []
    for d in range(1, heads):
        peer = lax.rem(h + d, heads)
        source, target = view(h, peer)
        at = base * heads + d
        copies.append(remote(source, target, send.at[at], recv.at[at], head=peer))
    source, target = view(h, h)
    return copies + [pltpu.make_async_copy(source, target, local.at[base])]


def start(copies):
    for c in copies:
        c.start()


def wait(copies):
    for c in copies:
        c.wait()


def to_heads(src, dst, tokens, width):
    return lambda a, b: (src.at[:, cols(b, width)], dst.at[rows(a, tokens), :])


def piece_in(src, dst, width, offset, size):
    nt = src.shape[0]
    return lambda a, b: (
        src.at[:, :, pl.ds(pl.multiple_of(b * width + offset, 128), size)],
        dst.at[pl.ds(a * nt, nt)],
    )


def to_tokens(src, dst, tokens, width):
    return lambda a, b: (src.at[rows(b, tokens), :], dst.at[:, cols(a, width)])


def piece_out(src, dst, tokens, width, offset, size, base):
    return lambda a, b: (
        src.at[rows(b, tokens), pl.ds(base, size)],
        dst.at[:, pl.ds(pl.multiple_of(a * width + offset, 128), size)],
    )


def kernel_in(n, heads, size, key, ids, pair, ids_all, send, recv, local, isend, irecv):
    s = lax.axis_index("seq")
    greet(n, heads)
    copies = exchange(
        piece_in(key, pair, key.shape[2] // heads, 0, size), heads, send, recv, local, 0
    )

    def idc(d):
        return remote(ids, ids_all.at[s], isend.at[d], irecv.at[d], seq=lax.rem(s + d, n))

    mine = pltpu.make_async_copy(ids, ids_all.at[s], local.at[1])
    start(copies)
    each(n, lambda d: idc(d).start())
    mine.start()
    each(n, lambda d: idc(d).wait())
    mine.wait()
    wait(copies)


def halo(n, low, high, got, send, recv, at=0):
    s = lax.axis_index("seq")
    up, down = 2 * at, 2 * at + 1
    here = pl.ds(at * low.shape[1], low.shape[1])
    return [
        remote(high, got.at[0, :, here], send.at[up], recv.at[up], seq=lax.rem(s + 1, n)),
        remote(low, got.at[1, :, here], send.at[down], recv.at[down], seq=lax.rem(s + n - 1, n)),
    ]


def far_first(n, make):
    def go(i, c):
        make(n // 2 + ((i + 1) // 2) * (2 * lax.rem(i, 2) - 1)).start()
        return c

    lax.fori_loop(0, n - 1, go, 0)


def random_piece(n, c, src_of, dst, size, send, recv):
    s = lax.axis_index("seq")

    def make(d):
        peer = lax.rem(s + d, n)
        return remote(
            src_of(peer), dst.at[s, :, pl.ds(c * size, size)], send.at[c * n + d],
            recv.at[c * n + d], seq=peer,
        )

    return make


class Shared:
    def __init__(self, n, src, here, mine, layer, done, every, sems):
        s = lax.axis_index("seq")
        gs, gr, ls, lr, fs, fr, loc = sems
        self.group = group = src.shape[0]
        self.layers = n // group
        self.me, self.level = lax.rem(s, group), s // group
        self.mine, self.layer, self.done, self.every, self.here = mine, layer, done, every, here
        self.step1 = [pltpu.make_async_copy(src.at[self.me], here.at[self.me], loc.at[0])]
        self.step3 = []
        for j in range(1, group):
            to = lax.rem(self.me + j, group)
            peer = self.level * group + to
            self.step1.append(remote(src.at[to], here.at[self.me], gs.at[j], gr.at[j], seq=peer))
            self.step3.append(remote(done, every.at[self.me], fs.at[j], fr.at[j], seq=peer))
        self.across = lambda j: remote(
            mine, layer.at[self.level], ls.at[j], lr.at[j],
            seq=lax.rem(self.level + j, self.layers) * group + self.me,
        )

    def middle(self, combine):
        wait(self.step1)
        part = combine(self.here)
        self.mine[...] = part
        self.layer[self.level] = part
        each(self.layers, lambda j: self.across(j).start())

    def finish(self, combine):
        each(self.layers, lambda j: self.across(j).wait())
        total = combine(self.layer)
        self.done[...] = total
        self.every[self.me] = total
        start(self.step3)


def kernel_fetch(n, heads, pieces, served, owners, owned_at, query, grad, key, value, first, ready,
                 qh, gh, incoming, halos, gall, *rest):
    landed, rest = (first,) + rest[: pieces - 1], rest[pieces - 1 :]
    outgoing, gsrc, ghere, gmine, glayer, gdone = rest[:6]
    send, recv, local, bs, br, hs, hr, *gsems = rest[6:]
    s = lax.axis_index("seq")
    tokens, width = query.shape[0], query.shape[1] // heads
    size = 2 * width // pieces
    nb = first.shape[0]
    half = pieces // 2
    greet(n, heads)
    moves = [[]]
    for c in range(1, pieces):
        src = key if c < half else value
        moves.append(exchange(
            piece_in(src, landed[c], width, (c % half) * size, size),
            heads, send, recv, local, c,
        ))
    blocks = [
        random_piece(n, c, (lambda p, c=c: (ready.at[p] if c == 0 else outgoing.at[c - 1, p])),
                     incoming, size, bs, br)
        for c in range(pieces)
    ]
    qmove = exchange(to_heads(query, qh, tokens, width), heads, send, recv, local, pieces)
    qmove += exchange(to_heads(grad, gh, tokens, width), heads, send, recv, local, pieces + 1)
    edges = []
    for c in range(pieces):
        edges += halo(n, landed[c].at[0], landed[c].at[nb - 1], halos, hs, hr, c)
    shared = Shared(n, gsrc, ghere, gmine, glayer, gdone, gall, gsems)
    for m in moves:
        start(m)
    far_first(n, blocks[0])
    start(qmove)
    keep = pltpu.make_async_copy(ready.at[s], incoming.at[s, :, pl.ds(0, size)],
                                 local.at[pieces + 2])
    keep.start()
    for c in range(1, pieces):
        wait(moves[c])
        at = pl.ds(c * size, size)

        def gather(i, carry):
            outgoing[c - 1, i] = landed[c][served[i]]
            return carry

        lax.fori_loop(0, n, gather, 0)
        incoming[s, :, at] = landed[c][served[s]]
        if c == pieces - 1:
            group = gsrc.shape[0]
            per = group // GLOBALS
            count = BLOCK // per
            for m in range(group):
                low = (m % per) * count
                for k in range(pieces):
                    gsrc[m, :, pl.ds(k * size, size)] = landed[k][
                        owned_at[m // per], pl.ds(low, count), :
                    ]
            start(shared.step1 + edges)
            mine = owners[shared.me * GLOBALS // group]
            shared.middle(lambda ref: ref[lax.rem(mine, group)])
        far_first(n, blocks[c])
    shared.finish(lambda ref: ref[mine // group])
    keep.wait()
    wait(edges + qmove + shared.step3)
    for c in range(pieces):
        each(n, lambda d: blocks[c](d).wait())


def kernel_return(n, heads, pieces, served, owners, owned_at, att, qg, sending, edge, gsend, wsum,
                  out, qout, kout, vout, returned, halos, gall, summed, ghere, gmine, glayer,
                  gdone, send, recv, local, bs, br, hs, hr, *gsems):
    s = lax.axis_index("seq")
    width = att.shape[1]
    tokens = att.shape[0] // heads
    nb = att.shape[0] // BLOCK
    size = 2 * width // pieces
    half = pieces // 2
    greet(n, heads)
    moves = [
        exchange(
            piece_out(summed, kout if c < half else vout, tokens, width, (c % half) * size, size,
                      c * size),
            heads, send, recv, local, c,
        )
        for c in range(pieces)
    ]
    blocks = [
        random_piece(n, c, lambda p, c=c: sending.at[p, :, pl.ds(c * size, size)], returned, size,
                     bs, br)
        for c in range(pieces)
    ]
    qmove = exchange(to_tokens(att, out, tokens, width), heads, send, recv, local, pieces)
    qmove += exchange(to_tokens(qg, qout, tokens, width), heads, send, recv, local, pieces + 1)
    edges = halo(n, edge.at[0], edge.at[1], halos, hs, hr)
    shared = Shared(n, gsend, ghere, gmine, glayer, gdone, gall, gsems)
    keep = pltpu.make_async_copy(sending.at[s], returned.at[s], local.at[pieces + 2])

    def combine(ref):
        def add(i, acc):
            return acc + ref[i].astype(jnp.float32)

        zero = jnp.zeros(ref.shape[1:], jnp.float32)
        return lax.fori_loop(0, ref.shape[0], add, zero).astype(jnp.bfloat16)

    start(shared.step1 + edges)
    far_first(n, blocks[0])
    start(qmove + [keep])
    shared.middle(combine)
    for c in range(1, pieces):
        far_first(n, blocks[c])
    shared.finish(combine)
    keep.wait()
    wait(edges + shared.step3)
    strip = 16
    per = shared.group // GLOBALS
    count = BLOCK // per

    def weight(cond):
        return jnp.where(cond, 1.0, 0.0).astype(jnp.float32)

    for c in range(pieces):
        each(n, lambda d: blocks[c](d).wait())
        at = pl.ds(c * size, size)

        def one_strip(t, carry):
            low = pl.multiple_of(t * strip, strip)
            here = pl.ds(low, strip)
            acc = [wsum[pl.ds(pl.multiple_of((j + 1) * BLOCK + low, strip), strip), at]
                   for j in range(nb)]
            acc[0] = acc[0] + halos[0, here, at].astype(jnp.float32)
            acc[-1] = acc[-1] + halos[1, here, at].astype(jnp.float32)
            for g in range(GLOBALS):
                inside = pl.ds(pl.multiple_of(lax.rem(low, count), strip), strip)
                extra = gall[g * per + low // count, inside, at].astype(jnp.float32)
                for j in range(nb):
                    hit = (owners[g] == s) & (owned_at[g] == j)
                    acc[j] = acc[j] + weight(hit) * extra

            def add(i, accs):
                x = returned[i, here, at].astype(jnp.float32)
                which = served[i]
                return tuple(accs[j] + weight(which == j) * x for j in range(nb))

            acc = lax.fori_loop(0, n, add, tuple(acc))
            for j in range(nb):
                summed[pl.ds(pl.multiple_of(j * BLOCK + low, strip), strip), at] = acc[j].astype(
                    jnp.bfloat16
                )
            return carry

        lax.fori_loop(0, BLOCK // strip, one_strip, 0)
        start(moves[c])
    wait(qmove)
    for m in moves:
        wait(m)


def dot(a, b, ca, cb):
    return lax.dot_general(a, b, (((ca,), (cb,)), ((), ())), preferred_element_type=jnp.float32)


def kernel_attend(n, lanes, pieces, slots, qh, gh, halos, incoming, gall, *rest):
    landed, rest = rest[:pieces], rest[pieces:]
    att, qg, wsum, edge, sending, gsum, pairs, keys, gacc = rest
    nb = qh.shape[0] // BLOCK
    width = qh.shape[1]
    s = lax.axis_index("seq")
    per = lanes // HEAD_DIM
    scale = jnp.asarray(HEAD_DIM ** (-0.5), jnp.bfloat16)
    pairs[pl.ds(0, BLOCK)] = halos[0]
    size = landed[0].shape[1]
    for c in range(pieces):
        pairs[pl.ds(BLOCK, nb * BLOCK), pl.ds(c * size, size)] = landed[c][...]
    pairs[pl.ds((nb + 1) * BLOCK, BLOCK)] = halos[1]
    keys[pl.ds((3 + RANDOM) * BLOCK, GLOBALS * BLOCK)] = gall[...]
    gacc[...] = jnp.zeros_like(gacc)
    wsum[...] = jnp.zeros_like(wsum)
    if n > RANDOM * nb:
        sending[...] = jnp.zeros_like(sending)
    lane_head = lax.broadcasted_iota(jnp.int32, (BLOCK, lanes), 1) // HEAD_DIM
    part = lax.broadcasted_iota(jnp.int32, (PARTS * BLOCK, 1), 0) // BLOCK

    def stack(x):
        zero = jnp.zeros_like(x)
        return jnp.concatenate([jnp.where(lane_head == j, x, zero) for j in range(per)], axis=0)

    def unstack(x):
        got = x[0:BLOCK]
        for j in range(1, per):
            got = jnp.where(lane_head == j, x[j * BLOCK : (j + 1) * BLOCK], got)
        return got

    def block(b, carry):
        here = pl.ds(pl.multiple_of(b * BLOCK, BLOCK), BLOCK)
        window = pl.ds(pl.multiple_of(b * BLOCK, BLOCK), 3 * BLOCK)
        keys[pl.ds(0, 3 * BLOCK)] = pairs[window]
        for r in range(RANDOM):
            keys[pl.ds((3 + r) * BLOCK, BLOCK)] = incoming[slots[b * RANDOM + r]]
        number = s * nb + b
        bad = ((part == 0) & (number == 0)) | ((part == 2) & (number == n * nb - 1))
        for g in range(width // lanes):
            at = pl.ds(g * lanes, lanes)
            vat = pl.ds(width + g * lanes, lanes)
            q = stack(qh[here, at]) * scale
            do = stack(gh[here, at])
            k = keys[:, at]
            v = keys[:, vat]
            scores = jnp.where(bad, MASKED, dot(k, q, 1, 1))
            raw = jnp.exp(scores - jnp.max(scores, axis=0, keepdims=True))
            probs = raw * (1.0 / jnp.sum(raw, axis=0, keepdims=True))
            half = probs.astype(jnp.bfloat16)
            pgrad = dot(v, do, 1, 1)
            delta = jnp.sum(half.astype(jnp.float32) * pgrad, axis=0, keepdims=True)
            ds = (probs * (pgrad - delta)).astype(jnp.bfloat16)
            att[here, at] = unstack(dot(half, v, 0, 0)).astype(jnp.bfloat16)
            qg[here, at] = (unstack(dot(ds, k, 0, 0)) * HEAD_DIM ** (-0.5)).astype(jnp.bfloat16)
            for x, y, to in ((ds, q, at), (half, do, vat)):
                grad = dot(x, y, 1, 0)
                wsum[window, to] += grad[: 3 * BLOCK]
                for r in range(RANDOM):
                    low = (3 + r) * BLOCK
                    sending[slots[b * RANDOM + r], :, to] = grad[low : low + BLOCK].astype(
                        jnp.bfloat16
                    )
                gacc[:, to] += grad[(3 + RANDOM) * BLOCK :]
        return carry

    lax.fori_loop(0, nb, block, 0)
    edge[0] = wsum[pl.ds(0, BLOCK)].astype(jnp.bfloat16)
    edge[1] = wsum[pl.ds((nb + 1) * BLOCK, BLOCK)].astype(jnp.bfloat16)
    gsum[...] = gacc[...].astype(jnp.bfloat16)


def body(n, heads, query_rows, key_rows, value_rows, out_grad, random_blocks, global_blocks):
    bf = jnp.bfloat16
    tokens, full = query_rows.shape
    width = full // heads
    total = tokens * heads
    nb = total // BLOCK
    me = lax.axis_index("seq")
    dma = pltpu.SemaphoreType.DMA
    sds = jax.ShapeDtypeStruct
    requests = RANDOM * nb
    flat = random_blocks.reshape(requests)
    ids = jnp.broadcast_to(jnp.pad(flat, (0, 128 - requests))[None], (8, 128))
    pieces = min(4, 2 * width // 128)
    size = 2 * width // pieces
    blocked = (tokens // BLOCK, BLOCK, full)
    key_blocks, value_blocks = key_rows.reshape(blocked), value_rows.reshape(blocked)
    first, ids_all = pl.pallas_call(
        partial(kernel_in, n, heads, size),
        out_shape=(sds((nb, BLOCK, size), bf), sds((n, 8, 128), jnp.int32)),
        in_specs=[HBM, VMEM],
        out_specs=(VMEM,) * 2,
        scratch_shapes=[dma((heads,)), dma((heads,)), dma((2,)), dma((n,)), dma((n,))],
        compiler_params=params(0),
        name="head_in",
    )(key_blocks, ids)
    asked = ids_all[:, 0, :requests]
    served = jnp.sum(jnp.where(asked // nb == me, asked % nb, 0), axis=1).astype(jnp.int32)
    owners = global_blocks // nb
    owned_at = global_blocks % nb
    ready = jnp.take(first, served, axis=0, mode="clip")
    group = 4
    layers = n // group
    chunk = GLOBALS * BLOCK // group
    slab = sds((n, BLOCK, 2 * width), bf)
    small = sds((group, chunk, 2 * width), bf)
    wide = (chunk, 2 * width)
    scratch = [
        pltpu.VMEM(small.shape, bf), pltpu.VMEM(wide, bf), pltpu.VMEM((layers,) + wide, bf),
        pltpu.VMEM(wide, bf),
        dma(((pieces + 2) * heads,)), dma(((pieces + 2) * heads,)), dma((pieces + 3,)),
        dma((pieces * n,)), dma((pieces * n,)), dma((2 * pieces,)), dma((2 * pieces,)),
        dma((group,)), dma((group,)), dma((layers,)), dma((layers,)), dma((group,)),
        dma((group,)), dma((1,)),
    ]
    edges = sds((2, BLOCK, 2 * width), bf)
    qh, gh, incoming, halos, gall, *landed = pl.pallas_call(
        partial(kernel_fetch, n, heads, pieces),
        out_shape=(sds((total, width), bf), sds((total, width), bf), slab, edges, small)
        + (sds((nb, BLOCK, size), bf),) * (pieces - 1),
        in_specs=[SMEM] * 3 + [HBM] * 4 + [VMEM] * 2,
        out_specs=(VMEM,) * (4 + pieces),
        scratch_shapes=[pltpu.VMEM((pieces - 1, n, BLOCK, size), bf), pltpu.VMEM(small.shape, bf)]
        + scratch,
        compiler_params=params(1),
        name="fetch",
    )(served, owners, owned_at, query_rows, out_grad, key_blocks, value_blocks, first, ready)
    gwide = (GLOBALS * BLOCK, 2 * width)
    att, qg, wsum, edge, sending, gsum = pl.pallas_call(
        partial(kernel_attend, n, min(256, width), pieces),
        out_shape=(
            sds((total, width), bf), sds((total, width), bf),
            sds(((nb + 2) * BLOCK, 2 * width), jnp.float32), edges, slab, sds(gwide, bf),
        ),
        in_specs=[SMEM] + [VMEM] * (5 + pieces),
        out_specs=(VMEM,) * 6,
        scratch_shapes=[
            pltpu.VMEM(((nb + 2) * BLOCK, 2 * width), bf),
            pltpu.VMEM((PARTS * BLOCK, 2 * width), bf),
            pltpu.VMEM(gwide, jnp.float32),
        ],
        compiler_params=pltpu.CompilerParams(vmem_limit_bytes=48 * 1024 * 1024),
        name="attend",
    )(flat // nb, qh, gh, halos, incoming, gall.reshape(gwide),
      *[x.reshape(total, size) for x in (first, *landed)])
    return pl.pallas_call(
        partial(kernel_return, n, heads, pieces),
        out_shape=(sds((tokens, full), bf),) * 4,
        in_specs=[SMEM] * 3 + [VMEM] * 6,
        out_specs=(VMEM,) * 4,
        scratch_shapes=[
            pltpu.VMEM(slab.shape, bf), pltpu.VMEM(edges.shape, bf), pltpu.VMEM(small.shape, bf),
            pltpu.VMEM((total, 2 * width), bf),
        ] + scratch,
        compiler_params=params(2),
        name="give_back",
    )(served, owners, owned_at, att, qg, sending, edge, gsum.reshape(group, chunk, 2 * width),
      wsum)


def solution(mesh):
    rows_spec = P(("seq", "head"), None)
    return jax.shard_map(
        partial(body, mesh.shape["seq"], mesh.shape["head"]),
        mesh=mesh,
        in_specs=(rows_spec,) * 4 + (P("seq", None), P()),
        out_specs=(rows_spec,) * 4,
        check_vma=False,
    )
```

```python
from functools import partial

import jax
import jax.numpy as jnp
from jax import lax
from jax.experimental import pallas as pl
from jax.experimental.pallas import tpu as pltpu
from jax.sharding import PartitionSpec as P

HEAD_DIM = 64
BLOCK = 64
RANDOM = 2
GLOBALS = 2
PARTS = 3 + RANDOM + GLOBALS
MASKED = -1e30
MESH = pl.DeviceIdType.MESH
VMEM = pl.BlockSpec(memory_space=pltpu.VMEM)
HBM = pl.BlockSpec(memory_space=pltpu.HBM)
SMEM = pl.BlockSpec(memory_space=pltpu.SMEM)


def params(cid):
    return pltpu.CompilerParams(
        collective_id=cid, has_side_effects=True, vmem_limit_bytes=24 * 1024 * 1024
    )


def greet(n, heads):
    s, h = lax.axis_index("seq"), lax.axis_index("head")
    barrier = pltpu.get_barrier_semaphore()
    if n > 0:

        def hello(d, c):
            pl.semaphore_signal(
                barrier, inc=1, device_id={"seq": lax.rem(s + d, n)}, device_id_type=MESH
            )
            return c

        lax.fori_loop(1, n, hello, 0)
    for d in range(1, heads):
        pl.semaphore_signal(
            barrier, inc=1, device_id={"head": lax.rem(h + d, heads)}, device_id_type=MESH
        )
    pl.semaphore_wait(barrier, max(n - 1, 0) + heads - 1)


def cols(index, width, base=0):
    return pl.ds(pl.multiple_of(base + index * width, 128), width)


def rows(index, count):
    return pl.ds(pl.multiple_of(index * count, 16), count)


def each(n, f):
    def step(d, c):
        f(d)
        return c

    lax.fori_loop(1, n, step, 0)


def remote(src, dst, send, recv, **where):
    return pltpu.make_async_remote_copy(
        src_ref=src, dst_ref=dst, send_sem=send, recv_sem=recv, device_id=where,
        device_id_type=MESH,
    )


def exchange(view, heads, send, recv, local, base):
    h = lax.axis_index("head")
    copies = []
    for d in range(1, heads):
        peer = lax.rem(h + d, heads)
        source, target = view(h, peer)
        at = base * heads + d
        copies.append(remote(source, target, send.at[at], recv.at[at], head=peer))
    source, target = view(h, h)
    return copies + [pltpu.make_async_copy(source, target, local.at[base])]


def start(copies):
    for c in copies:
        c.start()


def wait(copies):
    for c in copies:
        c.wait()


def to_heads(src, dst, tokens, width):
    return lambda a, b: (src.at[:, cols(b, width)], dst.at[rows(a, tokens), :])


def piece_in(src, dst, width, offset, size):
    nt = src.shape[0]
    return lambda a, b: (
        src.at[:, :, pl.ds(pl.multiple_of(b * width + offset, 128), size)],
        dst.at[pl.ds(a * nt, nt)],
    )


def to_tokens(src, dst, tokens, width):
    return lambda a, b: (src.at[rows(b, tokens), :], dst.at[:, cols(a, width)])


def piece_out(src, dst, tokens, width, offset, size, base):
    return lambda a, b: (
        src.at[rows(b, tokens), pl.ds(base, size)],
        dst.at[:, pl.ds(pl.multiple_of(a * width + offset, 128), size)],
    )


def kernel_in(n, heads, size, key, ids, pair, ids_all, send, recv, local, isend, irecv):
    s = lax.axis_index("seq")
    greet(n, heads)
    copies = exchange(
        piece_in(key, pair, key.shape[2] // heads, 0, size), heads, send, recv, local, 0
    )

    def idc(d):
        return remote(ids, ids_all.at[s], isend.at[d], irecv.at[d], seq=lax.rem(s + d, n))

    mine = pltpu.make_async_copy(ids, ids_all.at[s], local.at[1])
    start(copies)
    each(n, lambda d: idc(d).start())
    mine.start()
    each(n, lambda d: idc(d).wait())
    mine.wait()
    wait(copies)


def halo(n, low, high, got, send, recv, at=0):
    s = lax.axis_index("seq")
    up, down = 2 * at, 2 * at + 1
    here = pl.ds(at * low.shape[1], low.shape[1])
    return [
        remote(high, got.at[0, :, here], send.at[up], recv.at[up], seq=lax.rem(s + 1, n)),
        remote(low, got.at[1, :, here], send.at[down], recv.at[down], seq=lax.rem(s + n - 1, n)),
    ]


def far_first(n, make):
    def go(i, c):
        make(n // 2 + ((i + 1) // 2) * (2 * lax.rem(i, 2) - 1)).start()
        return c

    lax.fori_loop(0, n - 1, go, 0)


def random_piece(n, c, src_of, dst, size, send, recv):
    s = lax.axis_index("seq")

    def make(d):
        peer = lax.rem(s + d, n)
        return remote(
            src_of(peer), dst.at[s, :, pl.ds(c * size, size)], send.at[c * n + d],
            recv.at[c * n + d], seq=peer,
        )

    return make


class Shared:
    def __init__(self, n, src, here, mine, layer, done, every, sems):
        s = lax.axis_index("seq")
        gs, gr, ls, lr, fs, fr, loc = sems
        self.group = group = src.shape[0]
        self.layers = n // group
        self.me, self.level = lax.rem(s, group), s // group
        self.mine, self.layer, self.done, self.every, self.here = mine, layer, done, every, here
        self.step1 = [pltpu.make_async_copy(src.at[self.me], here.at[self.me], loc.at[0])]
        self.step3 = []
        for j in range(1, group):
            to = lax.rem(self.me + j, group)
            peer = self.level * group + to
            self.step1.append(remote(src.at[to], here.at[self.me], gs.at[j], gr.at[j], seq=peer))
            self.step3.append(remote(done, every.at[self.me], fs.at[j], fr.at[j], seq=peer))
        self.across = lambda j: remote(
            mine, layer.at[self.level], ls.at[j], lr.at[j],
            seq=lax.rem(self.level + j, self.layers) * group + self.me,
        )

    def middle(self, combine):
        wait(self.step1)
        part = combine(self.here)
        self.mine[...] = part
        self.layer[self.level] = part
        each(self.layers, lambda j: self.across(j).start())

    def finish(self, combine):
        each(self.layers, lambda j: self.across(j).wait())
        total = combine(self.layer)
        self.done[...] = total
        self.every[self.me] = total
        start(self.step3)


def kernel_fetch(n, heads, pieces, served, owners, owned_at, query, grad, key, value, first, ready,
                 qh, gh, incoming, halos, gall, *rest):
    landed, rest = (first,) + rest[: pieces - 1], rest[pieces - 1 :]
    outgoing, gsrc, ghere, gmine, glayer, gdone = rest[:6]
    send, recv, local, bs, br, hs, hr, *gsems = rest[6:]
    s = lax.axis_index("seq")
    tokens, width = query.shape[0], query.shape[1] // heads
    size = 2 * width // pieces
    nb = first.shape[0]
    half = pieces // 2
    greet(n, heads)
    moves = [[]]
    for c in range(1, pieces):
        src = key if c < half else value
        moves.append(exchange(
            piece_in(src, landed[c], width, (c % half) * size, size),
            heads, send, recv, local, c,
        ))
    blocks = [
        random_piece(n, c, (lambda p, c=c: (ready.at[p] if c == 0 else outgoing.at[c - 1, p])),
                     incoming, size, bs, br)
        for c in range(pieces)
    ]
    qmove = exchange(to_heads(query, qh, tokens, width), heads, send, recv, local, pieces)
    qmove += exchange(to_heads(grad, gh, tokens, width), heads, send, recv, local, pieces + 1)
    edges = []
    for c in range(pieces):
        edges += halo(n, landed[c].at[0], landed[c].at[nb - 1], halos, hs, hr, c)
    shared = Shared(n, gsrc, ghere, gmine, glayer, gdone, gall, gsems)
    for m in moves:
        start(m)
    far_first(n, blocks[0])
    start(qmove)
    keep = pltpu.make_async_copy(ready.at[s], incoming.at[s, :, pl.ds(0, size)],
                                 local.at[pieces + 2])
    keep.start()
    for c in range(1, pieces):
        wait(moves[c])
        at = pl.ds(c * size, size)

        def gather(i, carry):
            outgoing[c - 1, i] = landed[c][served[i]]
            return carry

        lax.fori_loop(0, n, gather, 0)
        incoming[s, :, at] = landed[c][served[s]]
        if c == pieces - 1:
            group = gsrc.shape[0]
            per = group // GLOBALS
            count = BLOCK // per
            for m in range(group):
                low = (m % per) * count
                for k in range(pieces):
                    gsrc[m, :, pl.ds(k * size, size)] = landed[k][
                        owned_at[m // per], pl.ds(low, count), :
                    ]
            start(shared.step1 + edges)
            mine = owners[shared.me * GLOBALS // group]
            shared.middle(lambda ref: ref[lax.rem(mine, group)])
        far_first(n, blocks[c])
    shared.finish(lambda ref: ref[mine // group])
    keep.wait()
    wait(edges + qmove + shared.step3)
    for c in range(pieces):
        each(n, lambda d: blocks[c](d).wait())


def kernel_return(n, heads, pieces, served, owners, owned_at, att, qg, sending, edge, gsend, wsum,
                  out, qout, kout, vout, returned, halos, gall, summed, ghere, gmine, glayer,
                  gdone, send, recv, local, bs, br, hs, hr, *gsems):
    s = lax.axis_index("seq")
    width = att.shape[1]
    tokens = att.shape[0] // heads
    nb = att.shape[0] // BLOCK
    size = 2 * width // pieces
    half = pieces // 2
    greet(n, heads)
    moves = [
        exchange(
            piece_out(summed, kout if c < half else vout, tokens, width, (c % half) * size, size,
                      c * size),
            heads, send, recv, local, c,
        )
        for c in range(pieces)
    ]
    blocks = [
        random_piece(n, c, lambda p, c=c: sending.at[p, :, pl.ds(c * size, size)], returned, size,
                     bs, br)
        for c in range(pieces)
    ]
    qmove = exchange(to_tokens(att, out, tokens, width), heads, send, recv, local, pieces)
    qmove += exchange(to_tokens(qg, qout, tokens, width), heads, send, recv, local, pieces + 1)
    edges = halo(n, edge.at[0], edge.at[1], halos, hs, hr)
    shared = Shared(n, gsend, ghere, gmine, glayer, gdone, gall, gsems)
    keep = pltpu.make_async_copy(sending.at[s], returned.at[s], local.at[pieces + 2])

    def combine(ref):
        def add(i, acc):
            return acc + ref[i].astype(jnp.float32)

        zero = jnp.zeros(ref.shape[1:], jnp.float32)
        return lax.fori_loop(0, ref.shape[0], add, zero).astype(jnp.bfloat16)

    start(shared.step1 + edges)
    far_first(n, blocks[0])
    start(qmove + [keep])
    shared.middle(combine)
    for c in range(1, pieces):
        far_first(n, blocks[c])
    shared.finish(combine)
    keep.wait()
    wait(edges + shared.step3)
    strip = 16
    per = shared.group // GLOBALS
    count = BLOCK // per

    def weight(cond):
        return jnp.where(cond, 1.0, 0.0).astype(jnp.float32)

    for c in range(pieces):
        each(n, lambda d: blocks[c](d).wait())
        at = pl.ds(c * size, size)

        def one_strip(t, carry):
            low = pl.multiple_of(t * strip, strip)
            here = pl.ds(low, strip)
            acc = [wsum[pl.ds(pl.multiple_of((j + 1) * BLOCK + low, strip), strip), at]
                   for j in range(nb)]
            acc[0] = acc[0] + halos[0, here, at].astype(jnp.float32)
            acc[-1] = acc[-1] + halos[1, here, at].astype(jnp.float32)
            for g in range(GLOBALS):
                inside = pl.ds(pl.multiple_of(lax.rem(low, count), strip), strip)
                extra = gall[g * per + low // count, inside, at].astype(jnp.float32)
                for j in range(nb):
                    hit = (owners[g] == s) & (owned_at[g] == j)
                    acc[j] = acc[j] + weight(hit) * extra

            def add(i, accs):
                x = returned[i, here, at].astype(jnp.float32)
                which = served[i]
                return tuple(accs[j] + weight(which == j) * x for j in range(nb))

            acc = lax.fori_loop(0, n, add, tuple(acc))
            for j in range(nb):
                summed[pl.ds(pl.multiple_of(j * BLOCK + low, strip), strip), at] = acc[j].astype(
                    jnp.bfloat16
                )
            return carry

        lax.fori_loop(0, BLOCK // strip, one_strip, 0)
        start(moves[c])
    wait(qmove)
    for m in moves:
        wait(m)


def dot(a, b, ca, cb):
    return lax.dot_general(a, b, (((ca,), (cb,)), ((), ())), preferred_element_type=jnp.float32)


def kernel_attend(n, lanes, pieces, slots, qh, gh, halos, incoming, gall, *rest):
    landed, rest = rest[:pieces], rest[pieces:]
    att, qg, wsum, edge, sending, gsum, pairs, keys, gacc = rest
    nb = qh.shape[0] // BLOCK
    width = qh.shape[1]
    s = lax.axis_index("seq")
    per = lanes // HEAD_DIM
    scale = jnp.asarray(HEAD_DIM ** (-0.5), jnp.bfloat16)
    pairs[pl.ds(0, BLOCK)] = halos[0]
    size = landed[0].shape[1]
    for c in range(pieces):
        pairs[pl.ds(BLOCK, nb * BLOCK), pl.ds(c * size, size)] = landed[c][...]
    pairs[pl.ds((nb + 1) * BLOCK, BLOCK)] = halos[1]
    keys[pl.ds((3 + RANDOM) * BLOCK, GLOBALS * BLOCK)] = gall[...]
    gacc[...] = jnp.zeros_like(gacc)
    wsum[...] = jnp.zeros_like(wsum)
    if n > RANDOM * nb:
        sending[...] = jnp.zeros_like(sending)
    lane_head = lax.broadcasted_iota(jnp.int32, (BLOCK, lanes), 1) // HEAD_DIM
    part = lax.broadcasted_iota(jnp.int32, (PARTS * BLOCK, 1), 0) // BLOCK

    def stack(x):
        zero = jnp.zeros_like(x)
        return jnp.concatenate([jnp.where(lane_head == j, x, zero) for j in range(per)], axis=0)

    def unstack(x):
        got = x[0:BLOCK]
        for j in range(1, per):
            got = jnp.where(lane_head == j, x[j * BLOCK : (j + 1) * BLOCK], got)
        return got

    def block(b, carry):
        here = pl.ds(pl.multiple_of(b * BLOCK, BLOCK), BLOCK)
        window = pl.ds(pl.multiple_of(b * BLOCK, BLOCK), 3 * BLOCK)
        keys[pl.ds(0, 3 * BLOCK)] = pairs[window]
        for r in range(RANDOM):
            keys[pl.ds((3 + r) * BLOCK, BLOCK)] = incoming[slots[b * RANDOM + r]]
        number = s * nb + b
        bad = ((part == 0) & (number == 0)) | ((part == 2) & (number == n * nb - 1))
        for g in range(width // lanes):
            at = pl.ds(g * lanes, lanes)
            vat = pl.ds(width + g * lanes, lanes)
            q = stack(qh[here, at]) * scale
            do = stack(gh[here, at])
            k = keys[:, at]
            v = keys[:, vat]
            scores = jnp.where(bad, MASKED, dot(k, q, 1, 1))
            raw = jnp.exp(scores - jnp.max(scores, axis=0, keepdims=True))
            probs = raw * (1.0 / jnp.sum(raw, axis=0, keepdims=True))
            half = probs.astype(jnp.bfloat16)
            pgrad = dot(v, do, 1, 1)
            delta = jnp.sum(half.astype(jnp.float32) * pgrad, axis=0, keepdims=True)
            ds = (probs * (pgrad - delta)).astype(jnp.bfloat16)
            att[here, at] = unstack(dot(half, v, 0, 0)).astype(jnp.bfloat16)
            qg[here, at] = (unstack(dot(ds, k, 0, 0)) * HEAD_DIM ** (-0.5)).astype(jnp.bfloat16)
            for x, y, to in ((ds, q, at), (half, do, vat)):
                grad = dot(x, y, 1, 0)
                wsum[window, to] += grad[: 3 * BLOCK]
                for r in range(RANDOM):
                    low = (3 + r) * BLOCK
                    sending[slots[b * RANDOM + r], :, to] = grad[low : low + BLOCK].astype(
                        jnp.bfloat16
                    )
                gacc[:, to] += grad[(3 + RANDOM) * BLOCK :]
        return carry

    lax.fori_loop(0, nb, block, 0, unroll=2)
    edge[0] = wsum[pl.ds(0, BLOCK)].astype(jnp.bfloat16)
    edge[1] = wsum[pl.ds((nb + 1) * BLOCK, BLOCK)].astype(jnp.bfloat16)
    gsum[...] = gacc[...].astype(jnp.bfloat16)


def kernel_store(a, b, c, d, wa, wb, wc, wd, sem):
    copies = [
        pltpu.make_async_copy(x, y, sem.at[i])
        for i, (x, y) in enumerate(((a, wa), (b, wb), (c, wc), (d, wd)))
    ]
    start(copies)
    wait(copies)


def body(n, heads, query_rows, key_rows, value_rows, out_grad, random_blocks, global_blocks):
    bf = jnp.bfloat16
    tokens, full = query_rows.shape
    width = full // heads
    total = tokens * heads
    nb = total // BLOCK
    me = lax.axis_index("seq")
    dma = pltpu.SemaphoreType.DMA
    sds = jax.ShapeDtypeStruct
    requests = RANDOM * nb
    flat = random_blocks.reshape(requests)
    ids = jnp.broadcast_to(jnp.pad(flat, (0, 128 - requests))[None], (8, 128))
    pieces = min(4, 2 * width // 128)
    size = 2 * width // pieces
    blocked = (tokens // BLOCK, BLOCK, full)
    key_blocks, value_blocks = key_rows.reshape(blocked), value_rows.reshape(blocked)
    query_rows, key_blocks, value_blocks, out_grad = (
        pltpu.with_memory_space_constraint(x, pltpu.HBM)
        for x in (query_rows, key_blocks, value_blocks, out_grad)
    )
    first, ids_all = pl.pallas_call(
        partial(kernel_in, n, heads, size),
        out_shape=(sds((nb, BLOCK, size), bf), sds((n, 8, 128), jnp.int32)),
        in_specs=[HBM, VMEM],
        out_specs=(VMEM,) * 2,
        scratch_shapes=[dma((heads,)), dma((heads,)), dma((2,)), dma((n,)), dma((n,))],
        compiler_params=params(0),
        name="head_in",
    )(key_blocks, ids)
    asked = ids_all[:, 0, :requests]
    served = jnp.sum(jnp.where(asked // nb == me, asked % nb, 0), axis=1).astype(jnp.int32)
    owners = global_blocks // nb
    owned_at = global_blocks % nb
    ready = jnp.take(first, served, axis=0, mode="clip")
    group = 4
    layers = n // group
    chunk = GLOBALS * BLOCK // group
    slab = sds((n, BLOCK, 2 * width), bf)
    small = sds((group, chunk, 2 * width), bf)
    wide = (chunk, 2 * width)
    scratch = [
        pltpu.VMEM(small.shape, bf), pltpu.VMEM(wide, bf), pltpu.VMEM((layers,) + wide, bf),
        pltpu.VMEM(wide, bf),
        dma(((pieces + 2) * heads,)), dma(((pieces + 2) * heads,)), dma((pieces + 3,)),
        dma((pieces * n,)), dma((pieces * n,)), dma((2 * pieces,)), dma((2 * pieces,)),
        dma((group,)), dma((group,)), dma((layers,)), dma((layers,)), dma((group,)),
        dma((group,)), dma((1,)),
    ]
    edges = sds((2, BLOCK, 2 * width), bf)
    qh, gh, incoming, halos, gall, *landed = pl.pallas_call(
        partial(kernel_fetch, n, heads, pieces),
        out_shape=(sds((total, width), bf), sds((total, width), bf), slab, edges, small)
        + (sds((nb, BLOCK, size), bf),) * (pieces - 1),
        in_specs=[SMEM] * 3 + [HBM] * 4 + [VMEM] * 2,
        out_specs=(VMEM,) * (4 + pieces),
        scratch_shapes=[pltpu.VMEM((pieces - 1, n, BLOCK, size), bf), pltpu.VMEM(small.shape, bf)]
        + scratch,
        compiler_params=params(1),
        name="fetch",
    )(served, owners, owned_at, query_rows, out_grad, key_blocks, value_blocks, first, ready)
    gwide = (GLOBALS * BLOCK, 2 * width)
    att, qg, wsum, edge, sending, gsum = pl.pallas_call(
        partial(kernel_attend, n, min(256, width), pieces),
        out_shape=(
            sds((total, width), bf), sds((total, width), bf),
            sds(((nb + 2) * BLOCK, 2 * width), jnp.float32), edges, slab, sds(gwide, bf),
        ),
        in_specs=[SMEM] + [VMEM] * (5 + pieces),
        out_specs=(VMEM,) * 6,
        scratch_shapes=[
            pltpu.VMEM(((nb + 2) * BLOCK, 2 * width), bf),
            pltpu.VMEM((PARTS * BLOCK, 2 * width), bf),
            pltpu.VMEM(gwide, jnp.float32),
        ],
        compiler_params=pltpu.CompilerParams(vmem_limit_bytes=24 * 1024 * 1024),
        name="attend",
    )(flat // nb, qh, gh, halos, incoming, gall.reshape(gwide),
      *[x.reshape(total, size) for x in (first, *landed)])
    results = pl.pallas_call(
        partial(kernel_return, n, heads, pieces),
        out_shape=(sds((tokens, full), bf),) * 4,
        in_specs=[SMEM] * 3 + [VMEM] * 6,
        out_specs=(VMEM,) * 4,
        scratch_shapes=[
            pltpu.VMEM(slab.shape, bf), pltpu.VMEM(edges.shape, bf), pltpu.VMEM(small.shape, bf),
            pltpu.VMEM((total, 2 * width), bf),
        ] + scratch,
        compiler_params=params(2),
        name="give_back",
    )(served, owners, owned_at, att, qg, sending, edge, gsum.reshape(group, chunk, 2 * width),
      wsum)
    return pl.pallas_call(
        kernel_store,
        out_shape=(sds((tokens, full), bf),) * 4,
        in_specs=[VMEM] * 4,
        out_specs=(HBM,) * 4,
        scratch_shapes=[dma((4,))],
        compiler_params=pltpu.CompilerParams(vmem_limit_bytes=16 * 1024 * 1024),
        name="store",
    )(*results)


def solution(mesh):
    rows_spec = P(("seq", "head"), None)
    return jax.shard_map(
        partial(body, mesh.shape["seq"], mesh.shape["head"]),
        mesh=mesh,
        in_specs=(rows_spec,) * 4 + (P("seq", None), P()),
        out_specs=(rows_spec,) * 4,
        check_vma=False,
    )
```
